128 devices in a mesh: vocab: 8 (over x_lo, y), dp: 8 (over z, core), teacher: 2 (over x_hi).
Axes of the slice: x: 4 (x_hi: 2, x_lo: 2; x = x_hi * 2 + x_lo), y: 4, z: 4, core: 2. Of those that a mesh axis runs over, the one named last changes fastest.
Arguments:
- hidden_states: bfloat16 [2048, 4096], P('teacher'), may hold values from -300 to 300
- head_weight: bfloat16 [4096, 65536], P(None, ('vocab', 'dp')), may hold values from -3 to 3
- teacher_logits: bfloat16 [2048, 65536], P(None, ('vocab', 'dp', 'teacher')), may hold values from -20 to 460
- token_weight: float32 [2048], P('teacher'), may hold values from 2 to 20
Outputs:
- hidden_grad: bfloat16 [2048, 4096], P('teacher', ('vocab', 'dp'))
- weight_grad: bfloat16 [4096, 65536], P('teacher', ('vocab', 'dp'))
The draws below stay inside these ranges and needn't reach their ends.
All inputs are finite; a program needn't handle non-finite values.
Results may differ from the reference program's by a relative error of at most 0.005.
Values may be sent and summed in bfloat16 or wider, within the bound.
No kernel may reach another device: no remote copies, remote signals or barrier semaphores. Data moves between devices by JAX's collectives and lax.ppermute only.
A program may use at most 192 MiB of HBM per device.

```python
import math
import jax
import jax.numpy as jnp

D = 4096
TOKENS = 2048
V = 65536


def shared_weight(key):
    return jax.random.normal(jax.random.fold_in(key, 101), (D, V), jnp.float32) * (3.0 / math.sqrt(D))


def draw_head_weight(key, part):
    return shared_weight(key).astype(jnp.bfloat16)


def draw_hidden_states(key, part):
    states = jax.random.normal(jax.random.fold_in(key, 202), (TOKENS, D), jnp.float32)
    return states.astype(jnp.bfloat16)


def draw_teacher_logits(key, part):
    values = jax.random.normal(jax.random.fold_in(key, 404), (TOKENS, V), jnp.float32) * 3.0
    return values.astype(jnp.bfloat16)


def block_levels(rng, shape, pieces, smallest, high):
    factor_of = 1.0
    for dim, shards_of in pieces:
        steps = jax.random.uniform(jax.random.fold_in(jax.random.fold_in(rng, 6), dim), (shards_of,), jnp.float32, smallest / len(pieces), high / len(pieces))
        factor_of = factor_of * jnp.repeat(jnp.exp(steps), shape[dim] // shards_of).reshape((-1,) + (1,) * (len(shape) - 1 - dim))
    return factor_of


def setup_inputs(seed: int = 0) -> dict:
    key_of = jax.random.split(jax.random.key(seed), 5)
    hidden_states = draw_hidden_states(jax.random.fold_in(key_of[4], 71), 0)
    head_weight = draw_head_weight(jax.random.fold_in(key_of[4], 71), 0)
    teacher_logits = draw_teacher_logits(jax.random.fold_in(key_of[4], 71), 0)
    token_weight = jnp.clip(jnp.exp(math.log(20.0) - 2.3025851 * jax.random.uniform(key_of[3], (TOKENS,), jnp.float32) ** block_levels(key_of[3], (TOKENS,), ((0, 2),), -0.2, 0.2)), 2.0, 20.0)
    return {"hidden_states": hidden_states, "head_weight": head_weight, "teacher_logits": teacher_logits, "token_weight": token_weight}


def row_norm(values):
    top_value = jnp.max(values, axis=1, keepdims=True)
    return top_value + jnp.log(jnp.sum(jnp.exp(values - top_value), axis=1, keepdims=True))


def reference(hidden_states, head_weight, teacher_logits, token_weight):
    logits = jnp.dot(hidden_states, head_weight, preferred_element_type=jnp.float32)
    student_norm = row_norm(logits)
    teacher = teacher_logits.astype(jnp.float32)
    teacher_norm = row_norm(teacher)
    logit_grad = (token_weight[:, None] * (jnp.exp(logits - student_norm) - jnp.exp(teacher - teacher_norm))).astype(jnp.bfloat16)
    hidden_grad = jnp.dot(logit_grad, head_weight.T, preferred_element_type=jnp.float32).astype(jnp.bfloat16)
    weight_grad = jnp.dot(hidden_states.T, logit_grad, preferred_element_type=jnp.float32).astype(jnp.bfloat16)
    return hidden_grad, weight_grad
```

```python
import jax
import jax.numpy as jnp
from jax import lax
from jax.sharding import PartitionSpec as P

AXES = ("vocab", "dp", "teacher")
SHARDS = ("vocab", "dp")
BF16, F32 = jnp.bfloat16, jnp.float32


def pairs(move):
    out = []
    for x in range(2):
        for y in range(4):
            for z in range(4):
                for c in range(2):
                    for h in range(2):
                        a, b, d, e, g = move(x, y, z, c, h)
                        source = ((x * 4 + y) * 8 + z * 2 + c) * 2 + h
                        target = ((a * 4 + b % 4) * 8 + d % 4 * 2 + e) * 2 + g
                        out.append((source, target))
    return out


CORE = pairs(lambda x, y, z, c, h: (x, y, z, 1 - c, h))
LOW = pairs(lambda x, y, z, c, h: (1 - x, y, z, c, h))
HIGH = pairs(lambda x, y, z, c, h: (x, y, z, c, 1 - h))
Z = {k: pairs(lambda x, y, z, c, h, k=k: (x, y, z + k, c, h)) for k in (1, 2, 3)}
Y = {k: pairs(lambda x, y, z, c, h, k=k: (x, y + k, z, c, h)) for k in (1, 2, 3)}


def send(value, moves):
    return lax.ppermute(value, AXES, moves)


def pick(value, index, axis=0):
    return lax.dynamic_index_in_dim(value, index, axis, keepdims=False)


def dot(a, b, ca, cb, out=F32):
    return lax.dot_general(a, b, (((ca,), (cb,)), ((), ())), preferred_element_type=F32).astype(out)


def gather_stats(top, total):
    stats = jnp.stack([top, total])
    stats = jnp.broadcast_to(stats[None], (64,) + stats.shape)
    stats = lax.all_to_all(stats, SHARDS, 0, 0, tiled=True)
    tops, totals = stats[:, 0], stats[:, 1]
    best = jnp.max(tops, axis=0)
    return best + jnp.log(jnp.sum(totals * jnp.exp(tops - best), axis=0))


def per_device(hidden_states, head_weight, teacher_logits, token_weight):
    vocab, dp, high = (lax.axis_index(a) for a in AXES)
    low, y = vocab // 4, vocab % 4
    z, core = dp // 2, dp % 2

    shard = teacher_logits.reshape(2, 1024, 512)
    other_part = send(pick(shard, 1 - high), HIGH)
    own_part = pick(shard, high)
    shard32 = shard.astype(F32)
    top = jnp.max(shard32, axis=2)
    total = jnp.sum(jnp.exp(shard32 - top[:, :, None]), axis=2)
    theirs = send(jnp.stack([pick(top, 1 - high), pick(total, 1 - high)]), HIGH)
    top, total = pick(top, high), pick(total, high)
    best = jnp.maximum(top, theirs[0])
    total = total * jnp.exp(top - best) + theirs[1] * jnp.exp(theirs[0] - best)
    teacher_norm = gather_stats(best, total)

    piece = lax.dynamic_slice(hidden_states, (dp * 128, (1 - high) * 2048), (128, 2048))
    piece = send(piece, HIGH)
    other_hidden = lax.all_gather(piece, "dp", axis=0, tiled=True)

    logits = dot(hidden_states, head_weight, 1, 0)
    student_top = jnp.max(logits, axis=1)
    student_total = jnp.sum(jnp.exp(logits - student_top[:, None]), axis=1)
    student_norm = gather_stats(student_top, student_total)

    first = jnp.where(high == 0, own_part, other_part)
    second = jnp.where(high == 0, other_part, own_part)
    teacher = jnp.concatenate([first, second], axis=1).astype(F32)
    logit_grad = (
        token_weight[:, None]
        * (jnp.exp(logits - student_norm[:, None]) - jnp.exp(teacher - teacher_norm[:, None]))
    ).astype(BF16)
    other_grad = send(logit_grad, HIGH)

    rows = head_weight.reshape(2, 4, 4, 2, 64, 1024)
    theirs = pick(rows, 1 - core, 3).reshape(2, 1024, 1024)
    mine = pick(rows, core, 3).reshape(2, 1024, 1024)
    got = [send(dot(theirs[i], logit_grad, 1, 1, BF16), CORE) for i in range(2)]
    sums = []
    for i in range(2):
        here = dot(mine[i], logit_grad, 1, 1, BF16)
        sums.append((here.astype(F32) + got[i].astype(F32)).reshape(4, 4, 64, 1024))

    def exchange(value, axis, place, moves):
        arrived = [send(pick(value, (place + k) % 4, axis).astype(BF16), moves[k]) for k in (1, 2, 3)]
        return pick(value, place, axis) + sum(a.astype(F32) for a in arrived)

    a = exchange(sums[0], 1, z, Z)
    b = exchange(sums[1], 0, y, Y)
    a = exchange(a, 0, y, Y)
    b = exchange(b, 0, z, Z)
    arrived = send(jnp.where(low == 0, b, a).astype(BF16), LOW)
    hidden_grad = (jnp.where(low == 0, a, b) + arrived.astype(F32)).astype(BF16).T

    own_hidden = lax.dynamic_slice(hidden_states, (0, high * 2048), (1024, 2048))
    weight_grad = (dot(own_hidden, logit_grad, 0, 0) + dot(other_hidden, other_grad, 0, 0)).astype(BF16)
    return hidden_grad, weight_grad


def solution(mesh):
    return jax.shard_map(
        per_device,
        mesh=mesh,
        in_specs=(
            P("teacher", None),
            P(None, ("vocab", "dp")),
            P(None, ("vocab", "dp", "teacher")),
            P("teacher"),
        ),
        out_specs=(P("teacher", ("vocab", "dp")), P("teacher", ("vocab", "dp"))),
        check_vma=False,
    )
```

```python
import jax
import jax.numpy as jnp
from jax import lax
from jax.experimental.layout import Layout, with_layout_constraint
from jax.sharding import PartitionSpec as P


AXES = ("vocab", "dp", "teacher")
BF16, F32 = jnp.bfloat16, jnp.float32


def pairs(move):
    out = []
    for x in range(2):
        for y in range(4):
            for z in range(4):
                for c in range(2):
                    for h in range(2):
                        a, b, d, e, g = move(x, y, z, c, h)
                        source = ((x * 4 + y) * 8 + z * 2 + c) * 2 + h
                        target = ((a * 4 + b % 4) * 8 + d % 4 * 2 + e) * 2 + g
                        out.append((source, target))
    return out


CORE = pairs(lambda x, y, z, c, h: (x, y, z, 1 - c, h))
LOW = pairs(lambda x, y, z, c, h: (1 - x, y, z, c, h))
HIGH = pairs(lambda x, y, z, c, h: (x, y, z, c, 1 - h))
Z = {k: pairs(lambda x, y, z, c, h, k=k: (x, y, z + k, c, h)) for k in (1, 2, 3)}
Y = {k: pairs(lambda x, y, z, c, h, k=k: (x, y + k, z, c, h)) for k in (1, 2, 3)}


def send(value, moves):
    return lax.ppermute(value, AXES, moves)


def pick(value, index, axis=0):
    return lax.dynamic_index_in_dim(value, index, axis, keepdims=False)


def dot(a, b, ca, cb, out=F32):
    return lax.dot_general(a, b, (((ca,), (cb,)), ((), ())), preferred_element_type=F32).astype(out)


def merge(stats, axis):
    stats = jnp.broadcast_to(stats[None], (8,) + stats.shape)
    stats = lax.all_to_all(stats, axis, 0, 0, tiled=True)
    tops, totals = stats[:, 0], stats[:, 1]
    best = jnp.max(tops, axis=0)
    return best, jnp.sum(totals * jnp.exp(tops - best), axis=0)


def row_major(value):
    return with_layout_constraint(value, Layout(major_to_minor=(0, 1)))


def compute(hidden_states, head_weight, teacher_logits, token_weight):
    vocab, dp, high = (lax.axis_index(a) for a in AXES)
    low, y = vocab // 4, vocab % 4
    z, core = dp // 2, dp % 2

    part = row_major(lax.dynamic_slice(teacher_logits, ((1 - high) * 1024, 0), (1024, 512)))
    other_part = row_major(send(part, HIGH))
    own_part = lax.dynamic_slice(teacher_logits, (high * 1024, 0), (1024, 512))

    logits = dot(hidden_states, head_weight, 1, 0)
    student_top = jnp.max(logits, axis=1)
    student_total = jnp.sum(jnp.exp(logits - student_top[:, None]), axis=1)
    late, student_total = lax.optimization_barrier((dp, student_total))
    piece = lax.dynamic_slice(hidden_states, (late * 128, (1 - high) * 2048), (128, 2048))
    piece = send(piece, HIGH)
    other_hidden = lax.all_gather(piece, "dp", axis=0, tiled=True)
    student_top, student_total = merge(jnp.stack([student_top, student_total]), "dp")

    first = jnp.where(high == 0, own_part, other_part)
    second = jnp.where(high == 0, other_part, own_part)
    teacher = jnp.concatenate([first, second], axis=1).astype(F32)
    teacher_top = jnp.max(teacher, axis=1)
    teacher_total = jnp.sum(jnp.exp(teacher - teacher_top[:, None]), axis=1)
    teacher_top, teacher_total = merge(jnp.stack([teacher_top, teacher_total]), "dp")
    tops, totals = merge(
        jnp.stack([jnp.stack([student_top, teacher_top]), jnp.stack([student_total, teacher_total])]),
        "vocab",
    )
    student_norm, teacher_norm = tops + jnp.log(totals)

    logit_grad = (
        token_weight[:, None]
        * (jnp.exp(logits - student_norm[:, None]) - jnp.exp(teacher - teacher_norm[:, None]))
    ).astype(BF16)
    other_grad = send(logit_grad, HIGH)

    rows = head_weight.reshape(2, 4, 4, 2, 64, 1024)
    theirs = pick(rows, 1 - core, 3).reshape(2, 1024, 1024)
    mine = pick(rows, core, 3).reshape(2, 1024, 1024)

    def cross(i):
        value = dot(theirs[i], logit_grad, 1, 1, BF16)
        return send(value, CORE)

    def join(i, got):
        here = dot(mine[i], logit_grad, 1, 1)
        return (here + got.astype(F32)).astype(BF16).reshape(4, 4, 64, 1024)

    def exchange(value, axis, place, moves):
        arrived = [send(pick(value, (place + k) % 4, axis), moves[k]) for k in (1, 2, 3)]
        return pick(value, place, axis).astype(F32) + sum(a.astype(F32) for a in arrived)

    got = [cross(i) for i in range(2)]
    a, b = (join(i, got[i]) for i in range(2))
    a = exchange(a, 1, z, Z)
    b = exchange(b, 0, y, Y)
    a = exchange(a.astype(BF16), 0, y, Y)
    b = exchange(b.astype(BF16), 0, z, Z)
    arrived = send(jnp.where(low == 0, b, a).astype(BF16), LOW)
    hidden_grad = (jnp.where(low == 0, a, b) + arrived.astype(F32)).astype(BF16).T

    own_hidden = lax.dynamic_slice(hidden_states, (0, high * 2048), (1024, 2048))
    weight_grad = lax.optimization_barrier(dot(own_hidden, logit_grad, 0, 0))
    weight_grad = (weight_grad + dot(other_hidden, other_grad, 0, 0)).astype(BF16)
    return hidden_grad, weight_grad


def solution(mesh):
    return jax.shard_map(
        compute,
        mesh=mesh,
        in_specs=(
            P("teacher", None),
            P(None, ("vocab", "dp")),
            P(None, ("vocab", "dp", "teacher")),
            P("teacher"),
        ),
        out_specs=(P("teacher", ("vocab", "dp")), P("teacher", ("vocab", "dp"))),
        check_vma=False,
    )
```

```python
import jax
import jax.numpy as jnp
from jax import lax
from jax.experimental.layout import Layout, with_layout_constraint
from jax.sharding import PartitionSpec as P


AXES = ("vocab", "dp", "teacher")
BF16, F32 = jnp.bfloat16, jnp.float32


def pairs(move):
    out = []
    for x in range(2):
        for y in range(4):
            for z in range(4):
                for c in range(2):
                    for h in range(2):
                        a, b, d, e, g = move(x, y, z, c, h)
                        source = ((x * 4 + y) * 8 + z * 2 + c) * 2 + h
                        target = ((a * 4 + b % 4) * 8 + d % 4 * 2 + e) * 2 + g
                        out.append((source, target))
    return out


CORE = pairs(lambda x, y, z, c, h: (x, y, z, 1 - c, h))
LOW = pairs(lambda x, y, z, c, h: (1 - x, y, z, c, h))
HIGH = pairs(lambda x, y, z, c, h: (x, y, z, c, 1 - h))
Z = {k: pairs(lambda x, y, z, c, h, k=k: (x, y, z + k, c, h)) for k in (1, 2, 3)}
Y = {k: pairs(lambda x, y, z, c, h, k=k: (x, y + k, z, c, h)) for k in (1, 2, 3)}


def send(value, moves):
    return lax.ppermute(value, AXES, moves)


def pick(value, index, axis=0):
    return lax.dynamic_index_in_dim(value, index, axis, keepdims=False)


def dot(a, b, ca, cb, out=F32):
    return lax.dot_general(a, b, (((ca,), (cb,)), ((), ())), preferred_element_type=F32).astype(out)


def merge(stats, axis):
    stats = jnp.broadcast_to(stats[None], (8,) + stats.shape)
    stats = lax.all_to_all(stats, axis, 0, 0, tiled=True)
    tops, totals = stats[:, 0], stats[:, 1]
    best = jnp.max(tops, axis=0)
    return best, jnp.sum(totals * jnp.exp(tops - best), axis=0)


def row_major(value):
    return with_layout_constraint(value, Layout(major_to_minor=(0, 1)))


def compute(hidden_states, head_weight, teacher_logits, token_weight):
    vocab, dp, high = (lax.axis_index(a) for a in AXES)
    low, y = vocab // 4, vocab % 4
    z, core = dp // 2, dp % 2

    part = row_major(lax.dynamic_slice(teacher_logits, ((1 - high) * 1024, 0), (1024, 512)))
    other_part = row_major(send(part, HIGH))
    own_part = lax.dynamic_slice(teacher_logits, (high * 1024, 0), (1024, 512))

    logits = row_major(dot(hidden_states, head_weight, 1, 0))
    student_top = jnp.max(logits, axis=1)
    student_total = jnp.sum(jnp.exp(logits - student_top[:, None]), axis=1)
    first = jnp.where(high == 0, own_part, other_part)
    second = jnp.where(high == 0, other_part, own_part)
    teacher = jnp.concatenate([first, second], axis=1).astype(F32)
    teacher_top = jnp.max(teacher, axis=1)
    teacher_total = jnp.sum(jnp.exp(teacher - teacher_top[:, None]), axis=1)
    stats = jnp.stack(
        [jnp.stack([student_top, teacher_top]), jnp.stack([student_total, teacher_total])]
    )
    late_core, stats = lax.optimization_barrier((core, stats))
    stats = jnp.stack(merge(stats, "dp"))
    late_dp, stats = lax.optimization_barrier((dp, stats))
    rows = head_weight.reshape(2, 4, 4, 2, 64, 1024)
    own_rows = pick(rows, late_core, 3).reshape(2, 1024, 1024)
    theirs = pick(rows, 1 - late_core, 3).reshape(2048, 1024)
    own_rows, theirs, stats = lax.optimization_barrier((own_rows, theirs, stats))
    partner_rows = send(theirs, CORE).reshape(2, 1024, 1024)
    tops, totals = merge(stats, "vocab")

    piece = lax.dynamic_slice(hidden_states, (late_dp * 128, (1 - high) * 2048), (128, 2048))
    piece = send(piece, HIGH)
    piece, tops = lax.optimization_barrier((piece, tops))
    other_hidden = lax.all_gather(piece, "dp", axis=0, tiled=True)

    student_norm, teacher_norm = tops + jnp.log(totals)

    logit_grad = (
        token_weight[:, None]
        * (jnp.exp(logits - student_norm[:, None]) - jnp.exp(teacher - teacher_norm[:, None]))
    ).astype(BF16)
    partner_grad = send(logit_grad, CORE)
    other_grad = send(logit_grad, HIGH)

    def partial(i):
        here = lax.optimization_barrier(dot(own_rows[i], logit_grad, 1, 1))
        here = here + dot(partner_rows[i], partner_grad, 1, 1)
        return here.astype(BF16).reshape(4, 4, 64, 1024)

    def exchange(value, axis, place, moves):
        arrived = [send(pick(value, (place + k) % 4, axis), moves[k]) for k in (1, 2, 3)]
        return pick(value, place, axis).astype(F32) + sum(a.astype(F32) for a in arrived)

    a = exchange(partial(0), 1, z, Z)
    b = exchange(partial(1), 0, y, Y)
    a = exchange(a.astype(BF16), 0, y, Y)
    b = exchange(b.astype(BF16), 0, z, Z)
    arrived = send(jnp.where(low == 0, b, a).astype(BF16), LOW)
    hidden_grad = (jnp.where(low == 0, a, b) + arrived.astype(F32)).astype(BF16).T

    own_hidden = lax.dynamic_slice(hidden_states, (0, high * 2048), (1024, 2048))
    own_share = lax.optimization_barrier(dot(own_hidden, logit_grad, 0, 0))
    weight_grad = (own_share + dot(other_hidden, other_grad, 0, 0)).astype(BF16)
    return hidden_grad, weight_grad


def solution(mesh):
    return jax.shard_map(
        compute,
        mesh=mesh,
        in_specs=(
            P("teacher", None),
            P(None, ("vocab", "dp")),
            P(None, ("vocab", "dp", "teacher")),
            P("teacher"),
        ),
        out_specs=(P("teacher", ("vocab", "dp")), P("teacher", ("vocab", "dp"))),
        check_vma=False,
    )
```

```python
import jax
import jax.numpy as jnp
from jax import lax
from jax.experimental.layout import Layout, with_layout_constraint
from jax.sharding import PartitionSpec as P


AXES = ("vocab", "dp", "teacher")
BF16, F32 = jnp.bfloat16, jnp.float32


def pairs(move):
    out = []
    for x in range(2):
        for y in range(4):
            for z in range(4):
                for c in range(2):
                    for h in range(2):
                        a, b, d, e, g = move(x, y, z, c, h)
                        source = ((x * 4 + y) * 8 + z * 2 + c) * 2 + h
                        target = ((a * 4 + b % 4) * 8 + d % 4 * 2 + e) * 2 + g
                        out.append((source, target))
    return out


CORE = pairs(lambda x, y, z, c, h: (x, y, z, 1 - c, h))
LOW = pairs(lambda x, y, z, c, h: (1 - x, y, z, c, h))
HIGH = pairs(lambda x, y, z, c, h: (x, y, z, c, 1 - h))
Z = {k: pairs(lambda x, y, z, c, h, k=k: (x, y, z + k, c, h)) for k in (1, 2, 3)}
Y = {k: pairs(lambda x, y, z, c, h, k=k: (x, y + k, z, c, h)) for k in (1, 2, 3)}


def send(value, moves):
    return lax.ppermute(value, AXES, moves)


def pick(value, index, axis=0):
    return lax.dynamic_index_in_dim(value, index, axis, keepdims=False)


def dot(a, b, ca, cb, out=F32):
    return lax.dot_general(a, b, (((ca,), (cb,)), ((), ())), preferred_element_type=F32).astype(out)


def spread(stats):
    return jnp.broadcast_to(stats[None], (8,) + stats.shape)


def merge(stats, axis):
    stats = lax.all_to_all(stats, axis, 0, 0, tiled=True)
    tops, totals = stats[:, 0], stats[:, 1]
    best = jnp.max(tops, axis=0)
    return best, jnp.sum(totals * jnp.exp(tops - best), axis=0)


def row_major(value):
    return with_layout_constraint(value, Layout(major_to_minor=(0, 1)))


def compute(hidden_states, head_weight, teacher_logits, token_weight):
    vocab, dp, high = (lax.axis_index(a) for a in AXES)
    low, y = vocab // 4, vocab % 4
    z, core = dp // 2, dp % 2

    part = row_major(lax.dynamic_slice(teacher_logits, ((1 - high) * 1024, 0), (1024, 512)))
    other_part = row_major(send(part, HIGH))
    own_part = lax.dynamic_slice(teacher_logits, (high * 1024, 0), (1024, 512))

    logits = row_major(dot(hidden_states, head_weight, 1, 0))
    student_top = jnp.max(logits, axis=1)
    student_total = jnp.sum(jnp.exp(logits - student_top[:, None]), axis=1)
    late_dp, student_total = lax.optimization_barrier((dp, student_total))
    piece = lax.dynamic_slice(hidden_states, (late_dp * 128, (1 - high) * 2048), (128, 2048))
    piece = send(piece, HIGH)

    first = jnp.where(high == 0, own_part, other_part)
    second = jnp.where(high == 0, other_part, own_part)
    teacher = jnp.concatenate([first, second], axis=1).astype(F32)
    teacher_top = jnp.max(teacher, axis=1)
    teacher_total = jnp.sum(jnp.exp(teacher - teacher_top[:, None]), axis=1)
    stats = jnp.stack(
        [jnp.stack([student_top, teacher_top]), jnp.stack([student_total, teacher_total])]
    )
    late_core, stats = lax.optimization_barrier((core, spread(stats)))
    stats = jnp.stack(merge(stats, "dp"))
    piece, stats = lax.optimization_barrier((piece, stats))
    other_hidden = lax.all_gather(piece, "dp", axis=0, tiled=True)

    rows = head_weight.reshape(2, 4, 4, 2, 64, 1024)
    theirs = pick(rows, 1 - late_core, 3).reshape(2048, 1024)
    theirs, stats = lax.optimization_barrier((theirs, stats))
    partner_rows = send(theirs, CORE).reshape(2, 1024, 1024)
    stats = spread(stats)
    later_core, stats, _ = lax.optimization_barrier((core, stats, theirs))
    tops, totals = merge(stats, "vocab")
    own_rows = pick(rows, later_core, 3).reshape(2, 1024, 1024)
    own_rows, tops = lax.optimization_barrier((own_rows, tops))
    student_norm, teacher_norm = tops + jnp.log(totals)

    logit_grad = (
        token_weight[:, None]
        * (jnp.exp(logits - student_norm[:, None]) - jnp.exp(teacher - teacher_norm[:, None]))
    ).astype(BF16)
    partner_grad = send(logit_grad, CORE)
    other_grad = send(logit_grad, HIGH)

    def partial(i):
        here = lax.optimization_barrier(dot(own_rows[i], logit_grad, 1, 1))
        here = here + dot(partner_rows[i], partner_grad, 1, 1)
        return here.astype(BF16).reshape(4, 4, 64, 1024)

    def exchange(value, axis, place, moves):
        arrived = [send(pick(value, (place + k) % 4, axis), moves[k]) for k in (1, 2, 3)]
        return pick(value, place, axis).astype(F32) + sum(a.astype(F32) for a in arrived)

    a = exchange(partial(0), 1, z, Z)
    b = exchange(partial(1), 0, y, Y)
    a = exchange(a.astype(BF16), 0, y, Y)
    b = exchange(b.astype(BF16), 0, z, Z)
    arrived = send(jnp.where(low == 0, b, a).astype(BF16), LOW)
    hidden_grad = (jnp.where(low == 0, a, b) + arrived.astype(F32)).astype(BF16).T

    own_hidden = lax.dynamic_slice(hidden_states, (0, high * 2048), (1024, 2048))
    own_share = lax.optimization_barrier(dot(own_hidden, logit_grad, 0, 0))
    weight_grad = (own_share + dot(other_hidden, other_grad, 0, 0)).astype(BF16)
    return hidden_grad, weight_grad


def solution(mesh):
    return jax.shard_map(
        compute,
        mesh=mesh,
        in_specs=(
            P("teacher", None),
            P(None, ("vocab", "dp")),
            P(None, ("vocab", "dp", "teacher")),
            P("teacher"),
        ),
        out_specs=(P("teacher", ("vocab", "dp")), P("teacher", ("vocab", "dp"))),
        check_vma=False,
    )
```

```python
import jax
import jax.numpy as jnp
from jax import lax
from jax.experimental.layout import Layout, with_layout_constraint
from jax.sharding import PartitionSpec as P


AXES = ("vocab", "dp", "teacher")
BF16, F32 = jnp.bfloat16, jnp.float32
LOWEST = float(jnp.finfo(jnp.float32).min)


def pairs(move):
    out = []
    for x in range(2):
        for y in range(4):
            for z in range(4):
                for c in range(2):
                    for h in range(2):
                        a, b, d, e, g = move(x, y, z, c, h)
                        source = ((x * 4 + y) * 8 + z * 2 + c) * 2 + h
                        target = ((a * 4 + b % 4) * 8 + d % 4 * 2 + e) * 2 + g
                        out.append((source, target))
    return out


CORE = pairs(lambda x, y, z, c, h: (x, y, z, 1 - c, h))
LOW = pairs(lambda x, y, z, c, h: (1 - x, y, z, c, h))
HIGH = pairs(lambda x, y, z, c, h: (x, y, z, c, 1 - h))
Z = {k: pairs(lambda x, y, z, c, h, k=k: (x, y, z + k, c, h)) for k in (1, 2, 3)}
Y = {k: pairs(lambda x, y, z, c, h, k=k: (x, y + k, z, c, h)) for k in (1, 2, 3)}


def send(value, moves):
    return lax.ppermute(value, AXES, moves)


def pick(value, index, axis=0):
    return lax.dynamic_index_in_dim(value, index, axis, keepdims=False)


def dot(a, b, ca, cb, out=F32):
    return lax.dot_general(a, b, (((ca,), (cb,)), ((), ())), preferred_element_type=F32).astype(out)


def merge(stats, axis):
    stats = lax.all_to_all(stats, axis, 0, 0, tiled=True)
    tops, totals = stats[:, 0], stats[:, 1]
    best = jnp.max(tops, axis=0)
    return best, jnp.sum(totals * jnp.exp(tops - best), axis=0)


def row_major(value):
    return with_layout_constraint(value, Layout(major_to_minor=(0, 1)))


def compute(hidden_states, head_weight, teacher_logits, token_weight):
    vocab, dp, high = (lax.axis_index(a) for a in AXES)
    low, y = vocab // 4, vocab % 4
    z, core = dp // 2, dp % 2

    piece = lax.dynamic_slice(hidden_states, (dp * 128, (1 - high) * 2048), (128, 2048))
    piece = send(piece, HIGH)

    part = row_major(lax.dynamic_slice(teacher_logits, ((1 - high) * 1024, 0), (1024, 512)))
    other_part = row_major(send(part, HIGH))
    own_part = lax.dynamic_slice(teacher_logits, (high * 1024, 0), (1024, 512))

    logits = row_major(dot(hidden_states, head_weight, 1, 0))
    student_top = jnp.max(logits, axis=1)
    student_total = jnp.sum(jnp.exp(logits - student_top[:, None]), axis=1)
    piece, student_total = lax.optimization_barrier((piece, student_total))
    other_hidden = lax.all_gather(piece, "dp", axis=0, tiled=True)

    shard = teacher_logits.astype(F32)
    teacher_top = jnp.max(shard, axis=1)
    teacher_total = jnp.sum(jnp.exp(shard - teacher_top[:, None]), axis=1)

    tops = jnp.concatenate([student_top, teacher_top]).reshape(3, 1024)
    totals = jnp.concatenate([student_total, teacher_total]).reshape(3, 1024)
    stats = jnp.broadcast_to(jnp.stack([tops, totals])[None], (8, 2, 3, 1024))
    late_core, stats = lax.optimization_barrier((core, stats))
    tops, totals = merge(stats, "dp")
    rows = []
    for h in range(2):
        here = high == h
        rows.append(
            jnp.stack(
                [
                    jnp.stack([jnp.where(here, tops[0], LOWEST), tops[1 + h]]),
                    jnp.stack([jnp.where(here, totals[0], 0.0), totals[1 + h]]),
                ]
            )
        )
    stats = jnp.stack(rows)
    rows = head_weight.reshape(2, 4, 4, 2, 64, 1024)
    theirs = pick(rows, 1 - late_core, 3).reshape(2048, 1024)
    theirs, stats = lax.optimization_barrier((theirs, stats))
    partner_rows = send(theirs, CORE).reshape(2, 1024, 1024)
    stats = jnp.broadcast_to(stats[None], (8,) + stats.shape).reshape(16, 2, 2, 1024)
    later_core, stats, _ = lax.optimization_barrier((core, stats, theirs))
    tops, totals = merge(stats, ("vocab", "teacher"))
    own_rows = pick(rows, later_core, 3).reshape(2, 1024, 1024)
    own_rows, tops = lax.optimization_barrier((own_rows, tops))
    student_norm, teacher_norm = tops + jnp.log(totals)
    first = jnp.where(high == 0, own_part, other_part)
    second = jnp.where(high == 0, other_part, own_part)
    teacher = jnp.concatenate([first, second], axis=1).astype(F32)

    logit_grad = (
        token_weight[:, None]
        * (jnp.exp(logits - student_norm[:, None]) - jnp.exp(teacher - teacher_norm[:, None]))
    ).astype(BF16)
    partner_grad = send(logit_grad, CORE)
    other_grad = send(logit_grad, HIGH)

    def partial(i):
        here = lax.optimization_barrier(dot(own_rows[i], logit_grad, 1, 1))
        here = here + dot(partner_rows[i], partner_grad, 1, 1)
        return here.astype(BF16).reshape(4, 4, 64, 1024)

    def exchange(value, axis, place, moves):
        arrived = [send(pick(value, (place + k) % 4, axis), moves[k]) for k in (1, 2, 3)]
        return pick(value, place, axis).astype(F32) + sum(a.astype(F32) for a in arrived)

    a = exchange(partial(0), 1, z, Z)
    b = exchange(partial(1), 0, y, Y)
    a = exchange(a.astype(BF16), 0, y, Y)
    b = exchange(b.astype(BF16), 0, z, Z)
    arrived = send(jnp.where(low == 0, b, a).astype(BF16), LOW)
    hidden_grad = (jnp.where(low == 0, a, b) + arrived.astype(F32)).astype(BF16).T

    own_hidden = lax.dynamic_slice(hidden_states, (0, high * 2048), (1024, 2048))
    own_share = lax.optimization_barrier(dot(own_hidden, logit_grad, 0, 0))
    weight_grad = jnp.zeros((2048, 1024), BF16)
    for i in range(2):
        part = slice(i * 1024, i * 1024 + 1024)
        half = (own_share[part] + dot(other_hidden[:, part], other_grad, 0, 0)).astype(BF16)
        weight_grad = lax.dynamic_update_slice(weight_grad, half, (i * 1024, 0))
        weight_grad = lax.optimization_barrier(weight_grad)
    return hidden_grad, weight_grad


def solution(mesh):
    return jax.shard_map(
        compute,
        mesh=mesh,
        in_specs=(
            P("teacher", None),
            P(None, ("vocab", "dp")),
            P(None, ("vocab", "dp", "teacher")),
            P("teacher"),
        ),
        out_specs=(P("teacher", ("vocab", "dp")), P("teacher", ("vocab", "dp"))),
        check_vma=False,
    )
```

```python
import jax
import jax.numpy as jnp
from jax import lax
from jax.experimental.layout import Layout, with_layout_constraint
from jax.sharding import PartitionSpec as P


AXES = ("vocab", "dp", "teacher")
BF16, F32 = jnp.bfloat16, jnp.float32


def pairs(move):
    out = []
    for x in range(2):
        for y in range(4):
            for z in range(4):
                for c in range(2):
                    for h in range(2):
                        a, b, d, e, g = move(x, y, z, c, h)
                        source = ((x * 4 + y) * 8 + z * 2 + c) * 2 + h
                        target = ((a * 4 + b % 4) * 8 + d % 4 * 2 + e) * 2 + g
                        out.append((source, target))
    return out


CORE = pairs(lambda x, y, z, c, h: (x, y, z, 1 - c, h))
LOW = pairs(lambda x, y, z, c, h: (1 - x, y, z, c, h))
HIGH = pairs(lambda x, y, z, c, h: (x, y, z, c, 1 - h))
Z = {k: pairs(lambda x, y, z, c, h, k=k: (x, y, z + k, c, h)) for k in (1, 2, 3)}
Y = {k: pairs(lambda x, y, z, c, h, k=k: (x, y + k, z, c, h)) for k in (1, 2, 3)}


def send(value, moves):
    return lax.ppermute(value, AXES, moves)


def pick(value, index, axis=0):
    return lax.dynamic_index_in_dim(value, index, axis, keepdims=False)


def dot(a, b, ca, cb, out=F32):
    return lax.dot_general(a, b, (((ca,), (cb,)), ((), ())), preferred_element_type=F32).astype(out)


def spread(stats):
    return jnp.broadcast_to(stats[None], (8,) + stats.shape)


def merge(stats, axis):
    stats = lax.all_to_all(stats, axis, 0, 0, tiled=True)
    tops, totals = stats[:, 0], stats[:, 1]
    best = jnp.max(tops, axis=0)
    return best, jnp.sum(totals * jnp.exp(tops - best), axis=0)


def row_major(value):
    return with_layout_constraint(value, Layout(major_to_minor=(0, 1)))


def compute(hidden_states, head_weight, teacher_logits, token_weight):
    vocab, dp, high = (lax.axis_index(a) for a in AXES)
    low, y = vocab // 4, vocab % 4
    z, core = dp // 2, dp % 2

    shard = teacher_logits.astype(F32)
    top = jnp.max(shard, axis=1)
    total = jnp.sum(jnp.exp(shard - top[:, None]), axis=1)
    stats = jnp.stack([top.reshape(2, 1024), total.reshape(2, 1024)], axis=1)
    theirs = send(jnp.where(high == 0, stats[1], stats[0]), HIGH)
    mine = jnp.where(high == 0, stats[0], stats[1])
    teacher_top = jnp.maximum(mine[0], theirs[0])
    teacher_total = mine[1] * jnp.exp(mine[0] - teacher_top) + theirs[1] * jnp.exp(theirs[0] - teacher_top)

    piece = lax.dynamic_slice(hidden_states, (dp * 128, (1 - high) * 2048), (128, 2048))
    piece = send(piece, HIGH)

    part = row_major(lax.dynamic_slice(teacher_logits, ((1 - high) * 1024, 0), (1024, 512)))
    other_part = row_major(send(part, HIGH))
    own_part = lax.dynamic_slice(teacher_logits, (high * 1024, 0), (1024, 512))

    logits = row_major(dot(hidden_states, head_weight, 1, 0))
    student_top = jnp.max(logits, axis=1)
    student_total = jnp.sum(jnp.exp(logits - student_top[:, None]), axis=1)
    piece, student_total = lax.optimization_barrier((piece, student_total))
    other_hidden = lax.all_gather(piece, "dp", axis=0, tiled=True)

    stats = jnp.stack(
        [jnp.stack([student_top, teacher_top]), jnp.stack([student_total, teacher_total])]
    )
    late_core, stats = lax.optimization_barrier((core, spread(stats)))
    stats = jnp.stack(merge(stats, "dp"))

    rows = head_weight.reshape(2, 4, 4, 2, 64, 1024)
    theirs = pick(rows, 1 - late_core, 3).reshape(2048, 1024)
    theirs, stats = lax.optimization_barrier((theirs, stats))
    partner_rows = send(theirs, CORE).reshape(2, 1024, 1024)
    later_core, stats, _ = lax.optimization_barrier((core, spread(stats), theirs))
    tops, totals = merge(stats, "vocab")
    own_rows = pick(rows, later_core, 3).reshape(2, 1024, 1024)
    own_rows, tops = lax.optimization_barrier((own_rows, tops))
    student_norm, teacher_norm = tops + jnp.log(totals)
    first = jnp.where(high == 0, own_part, other_part)
    second = jnp.where(high == 0, other_part, own_part)
    teacher = jnp.concatenate([first, second], axis=1).astype(F32)

    logit_grad = (
        token_weight[:, None]
        * (jnp.exp(logits - student_norm[:, None]) - jnp.exp(teacher - teacher_norm[:, None]))
    ).astype(BF16)
    partner_grad = send(logit_grad, CORE)
    other_grad = send(logit_grad, HIGH)

    def partial(i):
        here = lax.optimization_barrier(dot(own_rows[i], logit_grad, 1, 1))
        here = here + dot(partner_rows[i], partner_grad, 1, 1)
        return here.astype(BF16).reshape(4, 4, 64, 1024)

    def exchange(value, axis, place, moves):
        arrived = [send(pick(value, (place + k) % 4, axis), moves[k]) for k in (1, 2, 3)]
        return pick(value, place, axis).astype(F32) + sum(a.astype(F32) for a in arrived)

    a = exchange(partial(0), 1, z, Z)
    b = exchange(partial(1), 0, y, Y)
    a = exchange(a.astype(BF16), 0, y, Y)
    b = exchange(b.astype(BF16), 0, z, Z)
    arrived = send(jnp.where(low == 0, b, a).astype(BF16), LOW)
    hidden_grad = (jnp.where(low == 0, a, b) + arrived.astype(F32)).astype(BF16).T

    own_hidden = lax.dynamic_slice(hidden_states, (0, high * 2048), (1024, 2048))
    own_share = lax.optimization_barrier(dot(own_hidden, logit_grad, 0, 0))
    weight_grad = jnp.zeros((2048, 1024), BF16)
    for i in range(2):
        part = slice(i * 1024, i * 1024 + 1024)
        half = (own_share[part] + dot(other_hidden[:, part], other_grad, 0, 0)).astype(BF16)
        weight_grad = lax.dynamic_update_slice(weight_grad, half, (i * 1024, 0))
        weight_grad = lax.optimization_barrier(weight_grad)
    return hidden_grad, weight_grad


def solution(mesh):
    return jax.shard_map(
        compute,
        mesh=mesh,
        in_specs=(
            P("teacher", None),
            P(None, ("vocab", "dp")),
            P(None, ("vocab", "dp", "teacher")),
            P("teacher"),
        ),
        out_specs=(P("teacher", ("vocab", "dp")), P("teacher", ("vocab", "dp"))),
        check_vma=False,
    )
```

```python
import jax
import jax.numpy as jnp
from jax import lax
from jax.experimental.layout import Layout, with_layout_constraint
from jax.sharding import PartitionSpec as P


AXES = ("vocab", "dp", "teacher")
BF16, F32 = jnp.bfloat16, jnp.float32


def pairs(move):
    out = []
    for x in range(2):
        for y in range(4):
            for z in range(4):
                for c in range(2):
                    for h in range(2):
                        a, b, d, e, g = move(x, y, z, c, h)
                        source = ((x * 4 + y) * 8 + z * 2 + c) * 2 + h
                        target = ((a * 4 + b % 4) * 8 + d % 4 * 2 + e) * 2 + g
                        out.append((source, target))
    return out


CORE = pairs(lambda x, y, z, c, h: (x, y, z, 1 - c, h))
LOW = pairs(lambda x, y, z, c, h: (1 - x, y, z, c, h))
HIGH = pairs(lambda x, y, z, c, h: (x, y, z, c, 1 - h))
Z = {k: pairs(lambda x, y, z, c, h, k=k: (x, y, z + k, c, h)) for k in (1, 2, 3)}
Y = {k: pairs(lambda x, y, z, c, h, k=k: (x, y + k, z, c, h)) for k in (1, 2, 3)}


def send(value, moves):
    return lax.ppermute(value, AXES, moves)


def pick(value, index, axis=0):
    return lax.dynamic_index_in_dim(value, index, axis, keepdims=False)


def dot(a, b, ca, cb, out=F32):
    return lax.dot_general(a, b, (((ca,), (cb,)), ((), ())), preferred_element_type=F32).astype(out)


def spread(stats):
    return jnp.broadcast_to(stats[None], (8,) + stats.shape)


def merge(stats, axis):
    stats = lax.all_to_all(stats, axis, 0, 0, tiled=True)
    tops, totals = stats[:, 0], stats[:, 1]
    best = jnp.max(tops, axis=0)
    return best, jnp.sum(totals * jnp.exp(tops - best), axis=0)


def row_major(value):
    return with_layout_constraint(value, Layout(major_to_minor=(0, 1)))


def compute(hidden_states, head_weight, teacher_logits, token_weight):
    vocab, dp, high = (lax.axis_index(a) for a in AXES)
    low, y = vocab // 4, vocab % 4
    z, core = dp // 2, dp % 2

    shard = teacher_logits.astype(F32)
    top = jnp.max(shard, axis=1)
    total = jnp.sum(jnp.exp(shard - top[:, None]), axis=1)
    stats = jnp.stack([top.reshape(2, 1024), total.reshape(2, 1024)], axis=1)
    theirs = send(jnp.where(high == 0, stats[1], stats[0]), HIGH)
    mine = jnp.where(high == 0, stats[0], stats[1])
    teacher_top = jnp.maximum(mine[0], theirs[0])
    teacher_total = mine[1] * jnp.exp(mine[0] - teacher_top) + theirs[1] * jnp.exp(theirs[0] - teacher_top)

    piece = lax.dynamic_slice(hidden_states, (dp * 128, (1 - high) * 2048), (128, 2048))
    piece = send(piece, HIGH)

    part = row_major(lax.dynamic_slice(teacher_logits, ((1 - high) * 1024, 0), (1024, 512)))
    other_part = row_major(send(part, HIGH))
    own_part = lax.dynamic_slice(teacher_logits, (high * 1024, 0), (1024, 512))

    logits = row_major(dot(hidden_states, head_weight, 1, 0))
    student_top = jnp.max(logits, axis=1)
    student_total = jnp.sum(jnp.exp(logits - student_top[:, None]), axis=1)
    piece, student_total = lax.optimization_barrier((piece, student_total))
    other_hidden = lax.all_gather(piece, "dp", axis=0, tiled=True)

    stats = jnp.stack(
        [jnp.stack([student_top, teacher_top]), jnp.stack([student_total, teacher_total])]
    )
    late_core, stats = lax.optimization_barrier((core, spread(stats)))
    stats = jnp.stack(merge(stats, "dp"))

    rows = head_weight.reshape(2, 4, 4, 2, 64, 1024)
    theirs = pick(rows, 1 - late_core, 3).reshape(2048, 1024)
    theirs, stats = lax.optimization_barrier((theirs, stats))
    partner_rows = send(theirs, CORE)
    later_core, stats, _ = lax.optimization_barrier((core, spread(stats), theirs))
    tops, totals = merge(stats, "vocab")
    own_rows = pick(rows, later_core, 3).reshape(2048, 1024)
    own_rows, tops = lax.optimization_barrier((own_rows, tops))
    student_norm, teacher_norm = tops + jnp.log(totals)
    first = jnp.where(high == 0, own_part, other_part)
    second = jnp.where(high == 0, other_part, own_part)
    teacher = jnp.concatenate([first, second], axis=1).astype(F32)

    logit_grad = (
        token_weight[:, None]
        * (jnp.exp(logits - student_norm[:, None]) - jnp.exp(teacher - teacher_norm[:, None]))
    ).astype(BF16)
    partner_grad = send(logit_grad, CORE)
    other_grad = send(logit_grad, HIGH)

    tokens = (slice(0, 640), slice(640, 1024))

    def partial(i):
        here = lax.optimization_barrier(dot(own_rows, logit_grad[tokens[i]], 1, 1))
        here = here + dot(partner_rows, partner_grad[tokens[i]], 1, 1)
        return here.astype(BF16).reshape(2, 4, 4, 64, -1)

    def exchange(value, axis, place, moves):
        slabs = [pick(value, (place + k) % 4, axis) for k in (1, 2, 3)]
        slabs = [slab.reshape(-1, slab.shape[-1]) for slab in slabs]
        arrived = [send(slab, moves[k]) for k, slab in zip((1, 2, 3), slabs)]
        own = pick(value, place, axis)
        total = own.reshape(slabs[0].shape).astype(F32) + sum(a.astype(F32) for a in arrived)
        return total.reshape(own.shape)

    a = exchange(partial(0), 2, z, Z)
    b = exchange(partial(1), 1, y, Y)
    a = exchange(a.astype(BF16), 1, y, Y)
    b = exchange(b.astype(BF16), 1, z, Z)
    sums = jnp.concatenate([a, b], axis=2)
    arrived = send(jnp.where(low == 0, sums[1], sums[0]).astype(BF16), LOW)
    hidden_grad = (jnp.where(low == 0, sums[0], sums[1]) + arrived.astype(F32)).astype(BF16).T

    own_hidden = lax.dynamic_slice(hidden_states, (0, high * 2048), (1024, 2048))
    own_share = lax.optimization_barrier(dot(own_hidden, logit_grad, 0, 0))
    weight_grad = jnp.zeros((2048, 1024), BF16)
    for i in range(2):
        part = slice(i * 1024, i * 1024 + 1024)
        half = (own_share[part] + dot(other_hidden[:, part], other_grad, 0, 0)).astype(BF16)
        weight_grad = lax.dynamic_update_slice(weight_grad, half, (i * 1024, 0))
        weight_grad = lax.optimization_barrier(weight_grad)
    return hidden_grad, weight_grad


def solution(mesh):
    return jax.shard_map(
        compute,
        mesh=mesh,
        in_specs=(
            P("teacher", None),
            P(None, ("vocab", "dp")),
            P(None, ("vocab", "dp", "teacher")),
            P("teacher"),
        ),
        out_specs=(P("teacher", ("vocab", "dp")), P("teacher", ("vocab", "dp"))),
        check_vma=False,
    )
```

```python
import jax
import jax.numpy as jnp
from jax import lax
from jax.experimental import pallas as pl
from jax.experimental.layout import Layout, with_layout_constraint
from jax.sharding import PartitionSpec as P


AXES = ("vocab", "dp", "teacher")
BF16, F32 = jnp.bfloat16, jnp.float32


def pairs(move):
    out = []
    for x in range(2):
        for y in range(4):
            for z in range(4):
                for c in range(2):
                    for h in range(2):
                        a, b, d, e, g = move(x, y, z, c, h)
                        source = ((x * 4 + y) * 8 + z * 2 + c) * 2 + h
                        target = ((a * 4 + b % 4) * 8 + d % 4 * 2 + e) * 2 + g
                        out.append((source, target))
    return out


CORE = pairs(lambda x, y, z, c, h: (x, y, z, 1 - c, h))
LOW = pairs(lambda x, y, z, c, h: (1 - x, y, z, c, h))
HIGH = pairs(lambda x, y, z, c, h: (x, y, z, c, 1 - h))
Z = {k: pairs(lambda x, y, z, c, h, k=k: (x, y, z + k, c, h)) for k in (1, 2, 3)}
Y = {k: pairs(lambda x, y, z, c, h, k=k: (x, y + k, z, c, h)) for k in (1, 2, 3)}


def send(value, moves):
    return lax.ppermute(value, AXES, moves)


def pick(value, index, axis=0):
    return lax.dynamic_index_in_dim(value, index, axis, keepdims=False)


def dot(a, b, ca, cb, out=F32):
    return lax.dot_general(a, b, (((ca,), (cb,)), ((), ())), preferred_element_type=F32).astype(out)


def spread(stats):
    return jnp.broadcast_to(stats[None], (8,) + stats.shape)


def merge(stats, axis):
    stats = lax.all_to_all(stats, axis, 0, 0, tiled=True)
    tops, totals = stats[:, 0], stats[:, 1]
    best = jnp.max(tops, axis=0)
    return best, jnp.sum(totals * jnp.exp(tops - best), axis=0)


def stats_kernel(x_ref, out_ref):
    x = x_ref[...].astype(F32)
    top = jnp.max(x, axis=1, keepdims=True)
    total = jnp.sum(jnp.exp(x - top), axis=1, keepdims=True)
    lane = lax.broadcasted_iota(jnp.int32, (x.shape[0], 128), 1)
    out_ref[...] = jnp.where(lane == 0, top, total).T[:8]


def shard_stats(shard):
    tokens, columns = shard.shape
    out = pl.pallas_call(
        stats_kernel,
        grid=(4,),
        in_specs=[pl.BlockSpec((tokens // 4, columns), lambda i: (i, 0))],
        out_specs=pl.BlockSpec((8, tokens // 4), lambda i: (0, i)),
        out_shape=jax.ShapeDtypeStruct((8, tokens), F32),
        cost_estimate=pl.CostEstimate(flops=4 * tokens * columns, bytes_accessed=2 * tokens * columns, transcendentals=tokens * columns),
    )(shard)
    return out[:2]


def row_major(value):
    return with_layout_constraint(value, Layout(major_to_minor=(0, 1)))


def compute(hidden_states, head_weight, teacher_logits, token_weight):
    vocab, dp, high = (lax.axis_index(a) for a in AXES)
    low, y = vocab // 4, vocab % 4
    z, core = dp // 2, dp % 2

    stats = shard_stats(teacher_logits)
    stats = stats.reshape(2, 2, 1024).swapaxes(0, 1)
    theirs = send(jnp.where(high == 0, stats[1], stats[0]), HIGH)
    mine = jnp.where(high == 0, stats[0], stats[1])
    teacher_top = jnp.maximum(mine[0], theirs[0])
    teacher_total = mine[1] * jnp.exp(mine[0] - teacher_top) + theirs[1] * jnp.exp(theirs[0] - teacher_top)

    piece = lax.dynamic_slice(hidden_states, (dp * 128, (1 - high) * 2048), (128, 2048))
    piece = send(piece, HIGH)

    part = row_major(lax.dynamic_slice(teacher_logits, ((1 - high) * 1024, 0), (1024, 512)))
    other_part = row_major(send(part, HIGH))
    own_part = lax.dynamic_slice(teacher_logits, (high * 1024, 0), (1024, 512))

    logits = row_major(dot(hidden_states, head_weight, 1, 0))
    student_top = jnp.max(logits, axis=1)
    student_total = jnp.sum(jnp.exp(logits - student_top[:, None]), axis=1)
    piece, student_total = lax.optimization_barrier((piece, student_total))
    other_hidden = lax.all_gather(piece, "dp", axis=0, tiled=True)

    stats = jnp.stack(
        [jnp.stack([student_top, teacher_top]), jnp.stack([student_total, teacher_total])]
    )
    late_core, stats = lax.optimization_barrier((core, spread(stats)))
    stats = jnp.stack(merge(stats, "dp"))

    rows = head_weight.reshape(2, 4, 4, 2, 64, 1024)
    theirs = pick(rows, 1 - late_core, 3).reshape(2048, 1024)
    theirs, stats = lax.optimization_barrier((theirs, stats))
    partner_rows = send(theirs, CORE)
    later_core, stats, _ = lax.optimization_barrier((core, spread(stats), theirs))
    tops, totals = merge(stats, "vocab")
    own_rows = pick(rows, later_core, 3).reshape(2048, 1024)
    own_rows, tops = lax.optimization_barrier((own_rows, tops))
    student_norm, teacher_norm = tops + jnp.log(totals)
    first = jnp.where(high == 0, own_part, other_part)
    second = jnp.where(high == 0, other_part, own_part)
    teacher = jnp.concatenate([first, second], axis=1).astype(F32)

    logit_grad = (
        token_weight[:, None]
        * (jnp.exp(logits - student_norm[:, None]) - jnp.exp(teacher - teacher_norm[:, None]))
    ).astype(BF16)
    partner_grad = send(logit_grad, CORE)
    other_grad = send(logit_grad, HIGH)

    tokens = (slice(0, 640), slice(640, 1024))

    def partial(i):
        here = lax.optimization_barrier(dot(own_rows, logit_grad[tokens[i]], 1, 1))
        here = here + dot(partner_rows, partner_grad[tokens[i]], 1, 1)
        return here.astype(BF16).reshape(2, 4, 4, 64, -1)

    def exchange(value, axis, place, moves):
        slabs = [pick(value, (place + k) % 4, axis) for k in (1, 2, 3)]
        slabs = [slab.reshape(-1, slab.shape[-1]) for slab in slabs]
        arrived = [send(slab, moves[k]) for k, slab in zip((1, 2, 3), slabs)]
        own = pick(value, place, axis)
        total = own.reshape(slabs[0].shape).astype(F32) + sum(a.astype(F32) for a in arrived)
        return total.reshape(own.shape)

    a = exchange(partial(0), 2, z, Z)
    b = exchange(partial(1), 1, y, Y)
    a = exchange(a.astype(BF16), 1, y, Y)
    b = exchange(b.astype(BF16), 1, z, Z)
    sums = jnp.concatenate([a, b], axis=2)
    arrived = send(jnp.where(low == 0, sums[1], sums[0]).astype(BF16), LOW)
    hidden_grad = (jnp.where(low == 0, sums[0], sums[1]) + arrived.astype(F32)).astype(BF16).T

    own_hidden = lax.dynamic_slice(hidden_states, (0, high * 2048), (1024, 2048))
    own_share = lax.optimization_barrier(dot(own_hidden, logit_grad, 0, 0))
    weight_grad = jnp.zeros((2048, 1024), BF16)
    for i in range(2):
        part = slice(i * 1024, i * 1024 + 1024)
        half = (own_share[part] + dot(other_hidden[:, part], other_grad, 0, 0)).astype(BF16)
        weight_grad = lax.dynamic_update_slice(weight_grad, half, (i * 1024, 0))
        weight_grad = lax.optimization_barrier(weight_grad)
    return hidden_grad, weight_grad


def solution(mesh):
    return jax.shard_map(
        compute,
        mesh=mesh,
        in_specs=(
            P("teacher", None),
            P(None, ("vocab", "dp")),
            P(None, ("vocab", "dp", "teacher")),
            P("teacher"),
        ),
        out_specs=(P("teacher", ("vocab", "dp")), P("teacher", ("vocab", "dp"))),
        check_vma=False,
    )
```

```python
import jax
import jax.numpy as jnp
from jax import lax
from jax.experimental import pallas as pl
from jax.experimental.pallas import tpu as pltpu
from jax.experimental.layout import Layout, with_layout_constraint
from jax.sharding import PartitionSpec as P


AXES = ("vocab", "dp", "teacher")
BF16, F32 = jnp.bfloat16, jnp.float32


def pairs(move):
    out = []
    for x in range(2):
        for y in range(4):
            for z in range(4):
                for c in range(2):
                    for h in range(2):
                        a, b, d, e, g = move(x, y, z, c, h)
                        source = ((x * 4 + y) * 8 + z * 2 + c) * 2 + h
                        target = ((a * 4 + b % 4) * 8 + d % 4 * 2 + e) * 2 + g
                        out.append((source, target))
    return out


CORE = pairs(lambda x, y, z, c, h: (x, y, z, 1 - c, h))
LOW = pairs(lambda x, y, z, c, h: (1 - x, y, z, c, h))
HIGH = pairs(lambda x, y, z, c, h: (x, y, z, c, 1 - h))
Z = {k: pairs(lambda x, y, z, c, h, k=k: (x, y, z + k, c, h)) for k in (1, 2, 3)}
Y = {k: pairs(lambda x, y, z, c, h, k=k: (x, y + k, z, c, h)) for k in (1, 2, 3)}


def send(value, moves):
    return lax.ppermute(value, AXES, moves)


def pick(value, index, axis=0):
    return lax.dynamic_index_in_dim(value, index, axis, keepdims=False)


def dot(a, b, ca, cb, out=F32):
    return lax.dot_general(a, b, (((ca,), (cb,)), ((), ())), preferred_element_type=F32).astype(out)


def spread(stats):
    return jnp.broadcast_to(stats[None], (8,) + stats.shape)


def merge(stats, axis):
    stats = lax.all_to_all(stats, axis, 0, 0, tiled=True)
    tops, totals = stats[:, 0], stats[:, 1]
    best = jnp.max(tops, axis=0)
    return best, jnp.sum(totals * jnp.exp(tops - best), axis=0)


def stats_kernel(high_ref, x_ref, theirs_ref, mine_ref, part_ref):
    raw = x_ref[...]
    x = raw.astype(F32)
    top = jnp.max(x, axis=1, keepdims=True)
    total = jnp.sum(jnp.exp(x - top), axis=1, keepdims=True)
    lane = lax.broadcasted_iota(jnp.int32, (x.shape[0], 128), 1)
    stats = jnp.where(lane == 0, top, total).T[:8]
    step = pl.program_id(0)

    @pl.when(step < 2)
    def _():
        theirs_ref[...] = stats
        part_ref[...] = raw

    @pl.when(step >= 2)
    def _():
        mine_ref[...] = stats


def shard_stats(high, shard):
    first = lambda i, high_ref: (0, jnp.minimum(i, 1))
    last = lambda i, high_ref: (0, jnp.maximum(i - 2, 0))
    return pl.pallas_call(
        stats_kernel,
        grid_spec=pltpu.PrefetchScalarGridSpec(
            num_scalar_prefetch=1,
            grid=(4,),
            in_specs=[
                pl.BlockSpec(
                    (512, 512),
                    lambda i, high_ref: (jnp.where(i < 2, 2 - 2 * high_ref[0] + i, 2 * high_ref[0] + i - 2), 0),
                )
            ],
            out_specs=[
                pl.BlockSpec((8, 512), first),
                pl.BlockSpec((8, 512), last),
                pl.BlockSpec((512, 512), lambda i, high_ref: (jnp.minimum(i, 1), 0)),
            ],
        ),
        out_shape=[
            jax.ShapeDtypeStruct((8, 1024), F32),
            jax.ShapeDtypeStruct((8, 1024), F32),
            jax.ShapeDtypeStruct((1024, 512), BF16),
        ],
        cost_estimate=pl.CostEstimate(flops=4194304, bytes_accessed=3145728, transcendentals=1048576),
    )(high.astype(jnp.int32).reshape(1), shard)


def row_major(value):
    return with_layout_constraint(value, Layout(major_to_minor=(0, 1)))


def compute(hidden_states, head_weight, teacher_logits, token_weight):
    vocab, dp, high = (lax.axis_index(a) for a in AXES)
    low, y = vocab // 4, vocab % 4
    z, core = dp // 2, dp % 2

    other_stats, mine, part = shard_stats(high, teacher_logits)
    theirs = send(other_stats, HIGH)
    teacher_top = jnp.maximum(mine[0], theirs[0])
    teacher_total = mine[1] * jnp.exp(mine[0] - teacher_top) + theirs[1] * jnp.exp(theirs[0] - teacher_top)

    piece = lax.dynamic_slice(hidden_states, (dp * 128, (1 - high) * 2048), (128, 2048))
    piece = send(piece, HIGH)

    other_part = row_major(send(part, HIGH))
    own_part = lax.dynamic_slice(teacher_logits, (high * 1024, 0), (1024, 512))

    logits = row_major(dot(hidden_states, head_weight, 1, 0))
    student_top = jnp.max(logits, axis=1)
    student_total = jnp.sum(jnp.exp(logits - student_top[:, None]), axis=1)
    piece, student_total = lax.optimization_barrier((piece, student_total))
    other_hidden = lax.all_gather(piece, "dp", axis=0, tiled=True)

    stats = jnp.stack(
        [jnp.stack([student_top, teacher_top]), jnp.stack([student_total, teacher_total])]
    )
    late_core, stats = lax.optimization_barrier((core, spread(stats)))
    stats = jnp.stack(merge(stats, "dp"))

    rows = head_weight.reshape(2, 4, 4, 2, 64, 1024)
    theirs = pick(rows, 1 - late_core, 3).reshape(2048, 1024)
    theirs, stats = lax.optimization_barrier((theirs, stats))
    partner_rows = send(theirs, CORE)
    later_core, stats, _ = lax.optimization_barrier((core, spread(stats), theirs))
    tops, totals = merge(stats, "vocab")
    own_rows = pick(rows, later_core, 3).reshape(2048, 1024)
    own_rows, tops = lax.optimization_barrier((own_rows, tops))
    student_norm, teacher_norm = tops + jnp.log(totals)
    first = jnp.where(high == 0, own_part, other_part)
    second = jnp.where(high == 0, other_part, own_part)
    teacher = jnp.concatenate([first, second], axis=1).astype(F32)

    logit_grad = (
        token_weight[:, None]
        * (jnp.exp(logits - student_norm[:, None]) - jnp.exp(teacher - teacher_norm[:, None]))
    ).astype(BF16)
    partner_grad = send(logit_grad, CORE)
    other_grad = []
    for i in range(2):
        other_grad.append(send(logit_grad[:, i * 512 : i * 512 + 512], HIGH))

    tokens = (slice(0, 640), slice(640, 1024))

    def partial(i):
        here = lax.optimization_barrier(dot(own_rows, logit_grad[tokens[i]], 1, 1))
        here = here + dot(partner_rows, partner_grad[tokens[i]], 1, 1)
        return here.astype(BF16).reshape(2, 4, 4, 64, -1)

    def exchange(value, axis, place, moves):
        slabs = [pick(value, (place + k) % 4, axis) for k in (1, 2, 3)]
        slabs = [slab.reshape(-1, slab.shape[-1]) for slab in slabs]
        arrived = [send(slab, moves[k]) for k, slab in zip((1, 2, 3), slabs)]
        own = pick(value, place, axis)
        total = own.reshape(slabs[0].shape).astype(F32) + sum(a.astype(F32) for a in arrived)
        return total.reshape(own.shape)

    a = exchange(partial(0), 2, z, Z)
    b = exchange(partial(1), 1, y, Y)
    a = exchange(a.astype(BF16), 1, y, Y)
    b = exchange(b.astype(BF16), 1, z, Z)
    sums = jnp.concatenate([a, b], axis=2)
    arrived = send(jnp.where(low == 0, sums[1], sums[0]).astype(BF16), LOW)
    hidden_grad = (jnp.where(low == 0, sums[0], sums[1]) + arrived.astype(F32)).astype(BF16).T

    own_hidden = lax.dynamic_slice(hidden_states, (0, high * 2048), (1024, 2048))
    own_share = lax.optimization_barrier(dot(own_hidden, logit_grad, 0, 0))
    weight_grad = jnp.zeros((2048, 1024), BF16)
    for i in range(2):
        half = own_share[:, i * 512 : i * 512 + 512] + dot(other_hidden, other_grad[i], 0, 0)
        weight_grad = lax.dynamic_update_slice(weight_grad, half.astype(BF16), (0, i * 512))
        weight_grad = lax.optimization_barrier(weight_grad)
    return hidden_grad, weight_grad


def solution(mesh):
    return jax.shard_map(
        compute,
        mesh=mesh,
        in_specs=(
            P("teacher", None),
            P(None, ("vocab", "dp")),
            P(None, ("vocab", "dp", "teacher")),
            P("teacher"),
        ),
        out_specs=(P("teacher", ("vocab", "dp")), P("teacher", ("vocab", "dp"))),
        check_vma=False,
    )
```

```python
import jax
import jax.numpy as jnp
from jax import lax
from jax.experimental import pallas as pl
from jax.experimental.pallas import tpu as pltpu
from jax.experimental.layout import Layout, with_layout_constraint
from jax.sharding import PartitionSpec as P


AXES = ("vocab", "dp", "teacher")
BF16, F32 = jnp.bfloat16, jnp.float32


def pairs(move):
    out = []
    for x in range(2):
        for y in range(4):
            for z in range(4):
                for c in range(2):
                    for h in range(2):
                        a, b, d, e, g = move(x, y, z, c, h)
                        source = ((x * 4 + y) * 8 + z * 2 + c) * 2 + h
                        target = ((a * 4 + b % 4) * 8 + d % 4 * 2 + e) * 2 + g
                        out.append((source, target))
    return out


CORE = pairs(lambda x, y, z, c, h: (x, y, z, 1 - c, h))
LOW = pairs(lambda x, y, z, c, h: (1 - x, y, z, c, h))
HIGH = pairs(lambda x, y, z, c, h: (x, y, z, c, 1 - h))
Z = {k: pairs(lambda x, y, z, c, h, k=k: (x, y, z + k, c, h)) for k in (1, 2, 3)}
Y = {k: pairs(lambda x, y, z, c, h, k=k: (x, y + k, z, c, h)) for k in (1, 2, 3)}


def send(value, moves):
    return lax.ppermute(value, AXES, moves)


def pick(value, index, axis=0):
    return lax.dynamic_index_in_dim(value, index, axis, keepdims=False)


def dot(a, b, ca, cb, out=F32):
    return lax.dot_general(a, b, (((ca,), (cb,)), ((), ())), preferred_element_type=F32).astype(out)


def spread(stats):
    return jnp.broadcast_to(stats[None], (8,) + stats.shape)


def merge(stats, axis):
    stats = lax.all_to_all(stats, axis, 0, 0, tiled=True)
    tops, totals = stats[:, 0], stats[:, 1]
    best = jnp.max(tops, axis=0)
    return best, jnp.sum(totals * jnp.exp(tops - best), axis=0)


def stats_kernel(high_ref, x_ref, theirs_ref, mine_ref, part_ref):
    raw = x_ref[...]
    x = raw.astype(F32)
    top = jnp.max(x, axis=1, keepdims=True)
    total = jnp.sum(jnp.exp(x - top), axis=1, keepdims=True)
    lane = lax.broadcasted_iota(jnp.int32, (x.shape[0], 128), 1)
    stats = jnp.where(lane == 0, top, total).T[:8]
    step = pl.program_id(0)

    @pl.when(step < 2)
    def _():
        theirs_ref[...] = stats
        part_ref[...] = raw

    @pl.when(step >= 2)
    def _():
        mine_ref[...] = stats


def shard_stats(high, shard):
    first = lambda i, high_ref: (0, jnp.minimum(i, 1))
    last = lambda i, high_ref: (0, jnp.maximum(i - 2, 0))
    return pl.pallas_call(
        stats_kernel,
        grid_spec=pltpu.PrefetchScalarGridSpec(
            num_scalar_prefetch=1,
            grid=(4,),
            in_specs=[
                pl.BlockSpec(
                    (512, 512),
                    lambda i, high_ref: (jnp.where(i < 2, 2 - 2 * high_ref[0] + i, 2 * high_ref[0] + i - 2), 0),
                )
            ],
            out_specs=[
                pl.BlockSpec((8, 512), first),
                pl.BlockSpec((8, 512), last),
                pl.BlockSpec((512, 512), lambda i, high_ref: (jnp.minimum(i, 1), 0)),
            ],
        ),
        out_shape=[
            jax.ShapeDtypeStruct((8, 1024), F32),
            jax.ShapeDtypeStruct((8, 1024), F32),
            jax.ShapeDtypeStruct((1024, 512), BF16),
        ],
        cost_estimate=pl.CostEstimate(flops=4194304, bytes_accessed=3145728, transcendentals=1048576),
    )(high.astype(jnp.int32).reshape(1), shard)


def row_major(value):
    return with_layout_constraint(value, Layout(major_to_minor=(0, 1)))


def compute(hidden_states, head_weight, teacher_logits, token_weight):
    vocab, dp, high = (lax.axis_index(a) for a in AXES)
    low, y = vocab // 4, vocab % 4
    z, core = dp // 2, dp % 2

    other_stats, mine, part = shard_stats(high, teacher_logits)
    theirs = send(other_stats, HIGH)
    teacher_top = jnp.maximum(mine[0], theirs[0])
    teacher_total = mine[1] * jnp.exp(mine[0] - teacher_top) + theirs[1] * jnp.exp(theirs[0] - teacher_top)

    piece = lax.dynamic_slice(hidden_states, (dp * 128, (1 - high) * 2048), (128, 2048))
    piece = send(piece, HIGH)

    other_part = row_major(send(part, HIGH))
    own_part = lax.dynamic_slice(teacher_logits, (high * 1024, 0), (1024, 512))

    logits = row_major(dot(hidden_states, head_weight, 1, 0))
    student_top = jnp.max(logits, axis=1)
    student_total = jnp.sum(jnp.exp(logits - student_top[:, None]), axis=1)
    piece, student_total = lax.optimization_barrier((piece, student_total))
    other_hidden = lax.all_gather(piece, "dp", axis=0, tiled=True)

    stats = jnp.stack(
        [jnp.stack([student_top, teacher_top]), jnp.stack([student_total, teacher_total])]
    )
    late_core, stats = lax.optimization_barrier((core, spread(stats)))
    stats = jnp.stack(merge(stats, "dp"))

    rows = head_weight.reshape(2, 4, 4, 2, 64, 1024)
    theirs = pick(rows, 1 - late_core, 3).reshape(2048, 1024)
    theirs, stats = lax.optimization_barrier((theirs, stats))
    partner_rows = send(theirs, CORE)
    later_core, stats, _ = lax.optimization_barrier((core, spread(stats), theirs))
    tops, totals = merge(stats, "vocab")
    own_rows = pick(rows, later_core, 3).reshape(2048, 1024)
    own_rows, tops = lax.optimization_barrier((own_rows, tops))
    student_norm, teacher_norm = tops + jnp.log(totals)
    first = jnp.where(high == 0, own_part, other_part)
    second = jnp.where(high == 0, other_part, own_part)
    teacher = jnp.concatenate([first, second], axis=1).astype(F32)

    logit_grad = (
        token_weight[:, None]
        * (jnp.exp(logits - student_norm[:, None]) - jnp.exp(teacher - teacher_norm[:, None]))
    ).astype(BF16)
    partner_grad = send(logit_grad, CORE)
    other_grad = send(logit_grad, HIGH)

    tokens = (slice(0, 640), slice(640, 1024))

    def partial(i):
        here = lax.optimization_barrier(dot(own_rows, logit_grad[tokens[i]], 1, 1))
        here = here + dot(partner_rows, partner_grad[tokens[i]], 1, 1)
        return here.astype(BF16).reshape(2, 4, 4, 64, -1)

    def exchange(value, axis, place, moves):
        slabs = [pick(value, (place + k) % 4, axis) for k in (1, 2, 3)]
        slabs = [slab.reshape(-1, slab.shape[-1]) for slab in slabs]
        arrived = [send(slab, moves[k]) for k, slab in zip((1, 2, 3), slabs)]
        own = pick(value, place, axis)
        total = own.reshape(slabs[0].shape).astype(F32) + sum(a.astype(F32) for a in arrived)
        return total.reshape(own.shape)

    a = exchange(partial(0), 2, z, Z)
    b = exchange(partial(1), 1, y, Y)
    a = exchange(a.astype(BF16), 1, y, Y)
    b = exchange(b.astype(BF16), 1, z, Z)
    sums = jnp.concatenate([a, b], axis=2)
    arrived = send(jnp.where(low == 0, sums[1], sums[0]).astype(BF16), LOW)
    hidden_grad = (jnp.where(low == 0, sums[0], sums[1]) + arrived.astype(F32)).astype(BF16).T

    own_hidden = lax.dynamic_slice(hidden_states, (0, high * 2048), (1024, 2048))
    own_share = lax.optimization_barrier(dot(own_hidden, logit_grad, 0, 0))
    weight_grad = jnp.zeros((2048, 1024), BF16)
    for i in range(2):
        part = slice(i * 1024, i * 1024 + 1024)
        half = (own_share[part] + dot(other_hidden[:, part], other_grad, 0, 0)).astype(BF16)
        weight_grad = lax.dynamic_update_slice(weight_grad, half, (i * 1024, 0))
        weight_grad = lax.optimization_barrier(weight_grad)
    return hidden_grad, weight_grad


def solution(mesh):
    return jax.shard_map(
        compute,
        mesh=mesh,
        in_specs=(
            P("teacher", None),
            P(None, ("vocab", "dp")),
            P(None, ("vocab", "dp", "teacher")),
            P("teacher"),
        ),
        out_specs=(P("teacher", ("vocab", "dp")), P("teacher", ("vocab", "dp"))),
        check_vma=False,
    )
```

```python
import jax
import jax.numpy as jnp
from jax import lax
from jax.experimental import pallas as pl
from jax.experimental.pallas import tpu as pltpu
from jax.experimental.layout import Layout, with_layout_constraint
from jax.sharding import PartitionSpec as P


AXES = ("vocab", "dp", "teacher")
BF16, F32 = jnp.bfloat16, jnp.float32


def pairs(move):
    out = []
    for x in range(2):
        for y in range(4):
            for z in range(4):
                for c in range(2):
                    for h in range(2):
                        a, b, d, e, g = move(x, y, z, c, h)
                        source = ((x * 4 + y) * 8 + z * 2 + c) * 2 + h
                        target = ((a * 4 + b % 4) * 8 + d % 4 * 2 + e) * 2 + g
                        out.append((source, target))
    return out


CORE = pairs(lambda x, y, z, c, h: (x, y, z, 1 - c, h))
LOW = pairs(lambda x, y, z, c, h: (1 - x, y, z, c, h))
HIGH = pairs(lambda x, y, z, c, h: (x, y, z, c, 1 - h))
Z = {k: pairs(lambda x, y, z, c, h, k=k: (x, y, z + k, c, h)) for k in (1, 2, 3)}
Y = {k: pairs(lambda x, y, z, c, h, k=k: (x, y + k, z, c, h)) for k in (1, 2, 3)}


def send(value, moves):
    return lax.ppermute(value, AXES, moves)


def pick(value, index, axis=0):
    return lax.dynamic_index_in_dim(value, index, axis, keepdims=False)


def dot(a, b, ca, cb, out=F32):
    return lax.dot_general(a, b, (((ca,), (cb,)), ((), ())), preferred_element_type=F32).astype(out)


def spread(stats):
    return jnp.broadcast_to(stats[None], (8,) + stats.shape)


def merge(stats, axis):
    stats = lax.all_to_all(stats, axis, 0, 0, tiled=True)
    tops, totals = stats[:, 0], stats[:, 1]
    best = jnp.max(tops, axis=0)
    return best, jnp.sum(totals * jnp.exp(tops - best), axis=0)


def stats_kernel(high_ref, x_ref, theirs_ref, mine_ref, part_ref):
    raw = x_ref[...]
    x = raw.astype(F32)
    top = jnp.max(x, axis=1, keepdims=True)
    total = jnp.sum(jnp.exp(x - top), axis=1, keepdims=True)
    lane = lax.broadcasted_iota(jnp.int32, (x.shape[0], 128), 1)
    stats = jnp.where(lane == 0, top, total).T[:8]
    step = pl.program_id(0)

    @pl.when(step < 2)
    def _():
        high_part = stats.astype(BF16)
        rest = stats - high_part.astype(F32)
        middle = rest.astype(BF16)
        low_part = rest - middle.astype(F32)
        row = lax.broadcasted_iota(jnp.int32, stats.shape, 0)
        split = jnp.where(row == 2, middle.astype(F32), jnp.where(row == 3, low_part, high_part.astype(F32)))
        theirs_ref[...] = split.astype(BF16)
        part_ref[...] = raw

    @pl.when(step >= 2)
    def _():
        mine_ref[...] = stats


def shard_stats(high, shard):
    first = lambda i, high_ref: (0, jnp.minimum(i, 1))
    last = lambda i, high_ref: (0, jnp.maximum(i - 2, 0))
    return pl.pallas_call(
        stats_kernel,
        grid_spec=pltpu.PrefetchScalarGridSpec(
            num_scalar_prefetch=1,
            grid=(4,),
            in_specs=[
                pl.BlockSpec(
                    (512, 512),
                    lambda i, high_ref: (jnp.where(i < 2, 2 - 2 * high_ref[0] + i, 2 * high_ref[0] + i - 2), 0),
                )
            ],
            out_specs=[
                pl.BlockSpec((8, 512), first),
                pl.BlockSpec((8, 512), last),
                pl.BlockSpec((512, 512), lambda i, high_ref: (jnp.minimum(i, 1), 0)),
            ],
        ),
        out_shape=[
            jax.ShapeDtypeStruct((8, 1024), BF16),
            jax.ShapeDtypeStruct((8, 1024), F32),
            jax.ShapeDtypeStruct((1024, 512), BF16),
        ],
        cost_estimate=pl.CostEstimate(flops=4194304, bytes_accessed=3145728, transcendentals=1048576),
    )(high.astype(jnp.int32).reshape(1), shard)


def row_major(value):
    return with_layout_constraint(value, Layout(major_to_minor=(0, 1)))


def compute(hidden_states, head_weight, teacher_logits, token_weight):
    vocab, dp, high = (lax.axis_index(a) for a in AXES)
    low, y = vocab // 4, vocab % 4
    z, core = dp // 2, dp % 2

    other_stats, mine, part = shard_stats(high, teacher_logits)

    piece = lax.dynamic_slice(hidden_states, (dp * 128, (1 - high) * 2048), (128, 2048))
    piece = send(jnp.concatenate([piece, other_stats.reshape(4, 2048)[:4]], axis=0), HIGH)
    theirs = piece[128:].reshape(8, 1024)[:4].astype(F32)
    theirs = (theirs[0], theirs[1] + theirs[2] + theirs[3])
    piece = piece[:128]
    teacher_top = jnp.maximum(mine[0], theirs[0])
    teacher_total = mine[1] * jnp.exp(mine[0] - teacher_top) + theirs[1] * jnp.exp(theirs[0] - teacher_top)

    other_part = row_major(send(part, HIGH))
    own_part = lax.dynamic_slice(teacher_logits, (high * 1024, 0), (1024, 512))

    logits = row_major(dot(hidden_states, head_weight, 1, 0))
    student_top = jnp.max(logits, axis=1)
    student_total = jnp.sum(jnp.exp(logits - student_top[:, None]), axis=1)
    piece, student_total = lax.optimization_barrier((piece, student_total))
    other_hidden = lax.all_gather(piece, "dp", axis=0, tiled=True)

    stats = jnp.stack(
        [jnp.stack([student_top, teacher_top]), jnp.stack([student_total, teacher_total])]
    )
    late_core, stats = lax.optimization_barrier((core, spread(stats)))
    stats = jnp.stack(merge(stats, "dp"))

    rows = head_weight.reshape(2, 4, 4, 2, 64, 1024)
    theirs = pick(rows, 1 - late_core, 3).reshape(2048, 1024)
    theirs, stats = lax.optimization_barrier((theirs, stats))
    partner_rows = send(theirs, CORE)
    later_core, stats, _ = lax.optimization_barrier((core, spread(stats), theirs))
    tops, totals = merge(stats, "vocab")
    own_rows = pick(rows, later_core, 3).reshape(2048, 1024)
    own_rows, tops = lax.optimization_barrier((own_rows, tops))
    student_norm, teacher_norm = tops + jnp.log(totals)
    first = jnp.where(high == 0, own_part, other_part)
    second = jnp.where(high == 0, other_part, own_part)
    teacher = jnp.concatenate([first, second], axis=1).astype(F32)

    logit_grad = (
        token_weight[:, None]
        * (jnp.exp(logits - student_norm[:, None]) - jnp.exp(teacher - teacher_norm[:, None]))
    ).astype(BF16)
    partner_grad = send(logit_grad, CORE)
    other_grad = send(logit_grad, HIGH)

    tokens = (slice(0, 640), slice(640, 1024))

    def partial(i):
        here = lax.optimization_barrier(dot(own_rows, logit_grad[tokens[i]], 1, 1))
        here = here + dot(partner_rows, partner_grad[tokens[i]], 1, 1)
        return here.astype(BF16).reshape(2, 4, 4, 64, -1)

    def exchange(value, axis, place, moves):
        slabs = [pick(value, (place + k) % 4, axis) for k in (1, 2, 3)]
        slabs = [slab.reshape(-1, slab.shape[-1]) for slab in slabs]
        arrived = [send(slab, moves[k]) for k, slab in zip((1, 2, 3), slabs)]
        own = pick(value, place, axis)
        total = own.reshape(slabs[0].shape).astype(F32) + sum(a.astype(F32) for a in arrived)
        return total.reshape(own.shape)

    a = exchange(partial(0), 2, z, Z)
    b = exchange(partial(1), 1, y, Y)
    a = exchange(a.astype(BF16), 1, y, Y)
    b = exchange(b.astype(BF16), 1, z, Z)
    sums = jnp.concatenate([a, b], axis=2)
    arrived = send(jnp.where(low == 0, sums[1], sums[0]).astype(BF16), LOW)
    hidden_grad = (jnp.where(low == 0, sums[0], sums[1]) + arrived.astype(F32)).astype(BF16).T

    own_hidden = lax.dynamic_slice(hidden_states, (0, high * 2048), (1024, 2048))
    own_share = lax.optimization_barrier(dot(own_hidden, logit_grad, 0, 0))
    weight_grad = jnp.zeros((2048, 1024), BF16)
    for i in range(2):
        part = slice(i * 1024, i * 1024 + 1024)
        half = (own_share[part] + dot(other_hidden[:, part], other_grad, 0, 0)).astype(BF16)
        weight_grad = lax.dynamic_update_slice(weight_grad, half, (i * 1024, 0))
        weight_grad = lax.optimization_barrier(weight_grad)
    return hidden_grad, weight_grad


def solution(mesh):
    return jax.shard_map(
        compute,
        mesh=mesh,
        in_specs=(
            P("teacher", None),
            P(None, ("vocab", "dp")),
            P(None, ("vocab", "dp", "teacher")),
            P("teacher"),
        ),
        out_specs=(P("teacher", ("vocab", "dp")), P("teacher", ("vocab", "dp"))),
        check_vma=False,
    )
```
